32 devices in a mesh: group: 2 (over y), tm: 4 (over z), mp: 4 (over x, core).
Axes of the slice: x: 2, y: 2, z: 4, core: 2. Of those that a mesh axis runs over, the one named last changes fastest.
Arguments:
- tokens: bfloat16 [3072, 1536], P(('group', 'tm'), 'mp'), parts along dimension 0, may hold values from -6 to 6
- segment_ids: int32 [3072], P(('group', 'tm')), parts along dimension 0, may hold values from 0 to 7, never falling along the last dimension, each value on 1 to 1152 neighbouring positions
- ln_att_gain: float32 [1536], replicated, may hold values from 0.25 to 1.75
- w_query: bfloat16 [1536, 1536], P(None, 'mp'), may hold values from -3 to 3
- w_keyval: bfloat16 [1536, 2, 1536], P(None, None, 'mp'), may hold values from -0.15625 to 0.15625
- w_out: bfloat16 [1536, 1536], P('mp'), may hold values from -0.21875 to 0.21875
- ln_conv_gain: float32 [1536], replicated, may hold values from 0.25 to 1.75
- w_glu: bfloat16 [1536, 2, 1536], P(None, None, 'mp'), may hold values from -0.15625 to 0.15625
- w_depth: bfloat16 [31, 1536], P(None, 'mp'), may hold values from -1 to 1
- bn_scale: float32 [1536], P('mp'), may hold values from 0.5 to 2
- bn_shift: float32 [1536], P('mp'), may hold values from -3 to 3
- w_proj: bfloat16 [1536, 1536], P('mp'), may hold values from -0.21875 to 0.21875
Outputs:
- block_out: bfloat16 [3072, 1536], P(('group', 'tm'), 'mp'), parts along dimension 0
The draws below stay inside these ranges and needn't reach their ends.
There are 2 independent parts, one for each index of `group`. The reference program is written for one: setup_inputs(seed, part) draws one part's arguments, and reference() takes and returns one part's arrays. A program takes and returns all parts, laid end to end along the dimension named above; an argument that names none is the same for every part. Nothing has to cross between parts.
Inputs may be any that keep to these rules, and one draw needn't show every extreme that they name: `segment_ids`: non-decreasing along the frames; each of the 8 recordings has 1 to 1152 frames and one has exactly that many.
All inputs are finite; a program needn't handle non-finite values.
Results may differ from the reference program's by a relative error of at most 0.015.
The reference program's roundings to bfloat16 on the way (of `normed`, `context`, `middle`, `normed_conv`, `gated` and `swished`) count: a program that leaves them out, or rounds other values in their place, can miss the bound.
Values may be sent and summed in bfloat16 or wider, within the bound.
A program may use at most 64 MiB of HBM per device.

```python
import math
import jax
import jax.numpy as jnp
import numpy as np
from jax import lax

D = 1536
HEADS = 16
KERNEL = 31
SEGS = 8
TOK_DEV = 384
TOKENS = 1536
N_TM = 4
N_MP = 4


def draw_w_query(key, part):
    base = jnp.clip(jax.random.normal(key, (D, D), jnp.float32), -4.0, 4.0)
    return (base / math.sqrt(D)).astype(jnp.bfloat16)


def spiked(drawn, rng, source, target, shards_of, factor):
    def block_of(dim):
        return (jnp.arange(drawn.shape[dim]) // (drawn.shape[dim] // shards_of)).reshape((-1,) + (1,) * (drawn.ndim - 1 - dim))

    near = jax.random.permutation(rng, shards_of)[block_of(target)]
    far = (block_of(target) + shards_of // 2) % shards_of
    return jnp.where((block_of(source) == near) | (block_of(source) == far), factor * drawn, drawn)


def block_scale(own_key, dims, split, low, top_value):
    factor_of = 1.0
    for axis_at, shards_of in split:
        heights = jax.random.uniform(jax.random.fold_in(jax.random.fold_in(own_key, 6), axis_at), (shards_of,), jnp.float32, low / len(split), top_value / len(split))
        factor_of = factor_of * jnp.repeat(jnp.exp(heights), dims[axis_at] // shards_of).reshape((-1,) + (1,) * (len(dims) - 1 - axis_at))
    return factor_of


def split_up(amount, total, bound, lean):
    portions = [(1 << 20) // math.isqrt(standing ** lean) + 1 for standing in range(2, amount + 1)]
    surplus, counts = total - bound - (amount - 1), [1] * (amount - 1)
    while surplus > 0:
        movable = [i for i in range(amount - 1) if counts[i] < bound]
        pool, left = sum([portions[i] for i in movable]), surplus
        for i in movable:
            addition = min(bound - counts[i], max(1, left * portions[i] // pool), surplus)
            counts[i] = counts[i] + addition
            surplus = surplus - addition
    return np.array([bound] + counts)


def ragged_sizes(key, count, total, reach, slope):
    if count == 2:
        one = jax.random.randint(key, (), max(1, total - reach), min(reach, total - 1) + 1)
        return jnp.stack([one, total - one])
    lengths = jnp.asarray(split_up(count, total, reach, slope), jnp.int32)
    pairs = (count - 1) // 2
    donor, taker = lengths[1:1 + 2 * pairs:2], lengths[2:2 + 2 * pairs:2]
    margin = jnp.minimum(donor - 1, reach - taker)
    passed = jax.random.randint(jax.random.fold_in(key, 1), (pairs,), 0, 1 << 20) % (margin + 1)
    lengths = lengths.at[1:1 + 2 * pairs:2].set(donor - passed).at[2:2 + 2 * pairs:2].set(taker + passed)
    return lengths[jax.random.permutation(jax.random.fold_in(key, 2), count)]


def gaussian(key, dims, width, most, shards=(), held_as=jnp.bfloat16):
    array = jax.random.normal(key, dims, jnp.float32) * width
    if len(shards) > 0:
        array = block_scale(key, dims, shards, -0.22, 0.18) * array
    return jnp.clip(array, min=-most, max=most).astype(held_as)


def gaussian_with(rng, dims, scale, limit, shards, heavy, held_as=jnp.bfloat16):
    array = scale * jax.random.normal(rng, dims, jnp.float32)
    if shards:
        array = array * block_scale(rng, dims, shards, -0.22, 0.18)
    return jnp.clip(spiked(array, jax.random.fold_in(rng, 3), *heavy), -limit, limit).astype(held_as)


def setup_inputs(seed: int = 0, part: int = 0) -> dict:
    seeds = jax.random.split(jax.random.key(seed), 13)
    own_keys = jax.random.split(jax.random.fold_in(seeds[12], part), 13)
    tokens = gaussian(own_keys[0], (TOKENS, D), 1.0, 6.0, ((0, 4), (1, 4)))
    segment_ids = jnp.searchsorted(jnp.cumsum(ragged_sizes(own_keys[1], SEGS, TOKENS, 3 * TOKENS // 4, 0)), jnp.arange(TOKENS), side="right").astype(jnp.int32)
    ln_att_gain = jnp.clip(1.0 + 0.15 * jax.random.normal(seeds[2], (D,), jnp.float32), 0.25, 1.75)
    w_query = draw_w_query(jax.random.fold_in(seeds[12], 71), part)
    w_keyval = gaussian(seeds[4], (D, 2, D), D ** -0.5, 0.15625, ((2, 4),))
    w_out = gaussian_with(seeds[5], (D, D), D ** -0.5, 0.21875, ((0, 4),), (0, 1, 4, 2.0))
    ln_conv_gain = jnp.clip(1.0 + 0.15 * jax.random.normal(seeds[6], (D,), jnp.float32), 0.25, 1.75)
    w_glu = gaussian(seeds[7], (D, 2, D), D ** -0.5, 0.15625, ((2, 4),))
    w_depth = gaussian(seeds[8], (KERNEL, D), KERNEL ** -0.5, 1.0, ((1, 4),))
    bn_scale = jnp.clip(jnp.exp(math.log(2.0) - 1.3862944 * jax.random.uniform(seeds[9], (D,), jnp.float32) ** block_scale(seeds[9], (D,), ((0, 4),), -0.2, 0.2)), 0.5, 2.0)
    bn_shift = gaussian(seeds[10], (D,), 0.5, 3.0, ((0, 4),), jnp.float32)
    w_proj = gaussian_with(seeds[11], (D, D), D ** -0.5, 0.21875, ((0, 4),), (0, 1, 4, 2.0))
    return dict(tokens=tokens, segment_ids=segment_ids, ln_att_gain=ln_att_gain, w_query=w_query, w_keyval=w_keyval, w_out=w_out, ln_conv_gain=ln_conv_gain, w_glu=w_glu, w_depth=w_depth, bn_scale=bn_scale, bn_shift=bn_shift, w_proj=w_proj)


def layer_norm(values_in, gain_vec):
    row_mean = lax.optimization_barrier(jnp.mean(values_in, axis=-1, keepdims=True))
    centered = values_in - row_mean
    spread = lax.optimization_barrier(jnp.mean(centered * centered, axis=-1, keepdims=True))
    return centered * lax.rsqrt(spread + 1e-05) * gain_vec

def grouped_product(left, right):
    group_width = left.shape[1] // N_MP
    summed = jnp.zeros((left.shape[0], right.shape[1]), jnp.float32)
    for group_index in range(N_MP):
        lower = group_index * group_width
        partial_value = jnp.dot(left[:, lower:lower + group_width], right[lower:lower + group_width], preferred_element_type=jnp.float32)
        summed = summed + lax.optimization_barrier(partial_value.astype(jnp.bfloat16)).astype(jnp.float32)
    return summed

def reference(tokens, segment_ids, ln_att_gain, w_query, w_keyval, w_out, ln_conv_gain, w_glu, w_depth, bn_scale, bn_shift, w_proj):
    head_dim = D // HEADS
    score_scale = head_dim ** (-0.5)
    normed = layer_norm(tokens.astype(jnp.float32), ln_att_gain).astype(jnp.bfloat16)
    queries = jnp.dot(normed, w_query, preferred_element_type=jnp.float32).astype(jnp.bfloat16)
    key_part = jnp.dot(normed, w_keyval[:, 0, :], preferred_element_type=jnp.float32).astype(jnp.bfloat16)
    value_part = jnp.dot(normed, w_keyval[:, 1, :], preferred_element_type=jnp.float32).astype(jnp.bfloat16)

    def to_heads(matrix):
        return matrix.reshape(TOKENS, HEADS, head_dim).transpose(1, 0, 2)

    def head_attention(operands):
        q_head, k_head, v_head = operands

        def query_block(offset):
            q_rows = lax.dynamic_slice_in_dim(q_head, offset, TOK_DEV, 0)
            seg_rows = lax.dynamic_slice_in_dim(segment_ids, offset, TOK_DEV, 0)
            scores = jnp.dot(q_rows, k_head.T, preferred_element_type=jnp.float32) * score_scale
            same_seg = seg_rows[:, None] == segment_ids[None, :]
            scores = jnp.where(same_seg, scores, -jnp.inf)
            row_max = lax.optimization_barrier(jnp.max(scores, axis=1, keepdims=True))
            weights = jnp.exp(scores - row_max)
            weight_sum = lax.optimization_barrier(jnp.sum(weights, axis=1, keepdims=True))
            weighted = jnp.dot(weights.astype(jnp.bfloat16), v_head, preferred_element_type=jnp.float32)
            return (weighted / weight_sum).astype(jnp.bfloat16)
        offsets = (jnp.arange(N_TM) * TOK_DEV).astype(jnp.int32)
        return lax.map(query_block, offsets).reshape(TOKENS, head_dim)
    context = lax.map(head_attention, (to_heads(queries), to_heads(key_part), to_heads(value_part)))
    context = context.transpose(1, 0, 2).reshape(TOKENS, D)
    middle = (tokens.astype(jnp.float32) + grouped_product(context, w_out)).astype(jnp.bfloat16)
    normed_conv = layer_norm(middle.astype(jnp.float32), ln_conv_gain).astype(jnp.bfloat16)
    value_half = jnp.dot(normed_conv, w_glu[:, 0, :], preferred_element_type=jnp.float32)
    gate_half = jnp.dot(normed_conv, w_glu[:, 1, :], preferred_element_type=jnp.float32)
    gated = (value_half * jax.nn.sigmoid(gate_half)).astype(jnp.bfloat16)
    half_width = (KERNEL - 1) // 2
    padded = jnp.pad(gated.astype(jnp.float32), ((half_width, half_width), (0, 0)))
    padded_segs = jnp.pad(segment_ids, (half_width, half_width), constant_values=-1)
    depth = jnp.zeros((TOKENS, D), jnp.float32)
    for tap_index in range(KERNEL):
        same_seg = (padded_segs[tap_index:tap_index + TOKENS] == segment_ids)[:, None]
        shifted = jnp.where(same_seg, padded[tap_index:tap_index + TOKENS], 0.0)
        depth = depth + shifted * w_depth[tap_index].astype(jnp.float32)
    normalized = depth * bn_scale + bn_shift
    swished = (normalized * jax.nn.sigmoid(normalized)).astype(jnp.bfloat16)
    return (middle.astype(jnp.float32) + grouped_product(swished, w_proj)).astype(jnp.bfloat16)
```

```python
import functools

import jax
import jax.numpy as jnp
from jax import lax
from jax.experimental import pallas as pl
from jax.experimental.pallas import tpu as pltpu
from jax.sharding import PartitionSpec as P

HEAD_DIM = 96


def with_halo(value, sides, width):
    for axis, dim in sides:
        count, length = (lax.axis_size(axis), value.shape[dim])
        up = [(i, (i + 1) % count) for i in range(count - 1)]
        down = [(j, i) for i, j in up]
        last = lax.slice_in_dim(value, length - width, length, axis=dim)
        initial = lax.slice_in_dim(value, 0, width, axis=dim)
        before = lax.ppermute(last, axis, up)
        after = lax.ppermute(initial, axis, down)
        value = jnp.concatenate([before, value, after], axis=dim)
    return value


def layer_norm(values_in, gain_vec):
    row_mean = jnp.mean(values_in, axis=-1, keepdims=True)
    centered = values_in - row_mean
    spread = jnp.mean(centered * centered, axis=-1, keepdims=True)
    return centered * lax.rsqrt(spread + 1e-05) * gain_vec


def fold_keys(carry_state, query_heads, query_segs, keyval, key_segs, local_cols, score_scale):
    row_max, weight_sum, weighted = carry_state
    key_rows = keyval.shape[0]
    heads_here = query_heads.shape[1]
    key_part = keyval[:, :local_cols].reshape(key_rows, heads_here, -1)
    value_part = keyval[:, local_cols:].reshape(key_rows, heads_here, -1)
    scores = (
        jnp.einsum("qhd,khd->qhk", query_heads, key_part, preferred_element_type=jnp.float32)
        * score_scale
    )
    same_seg = (query_segs[:, None] == key_segs[None, :])[:, None, :]
    scores = jnp.where(same_seg, scores, -jnp.inf)
    new_max = jnp.maximum(row_max, jnp.max(scores, axis=2))
    safe_max = jnp.where(new_max == -jnp.inf, 0.0, new_max)
    weights = jnp.exp(scores - safe_max[:, :, None])
    factor = jnp.exp(row_max - safe_max)
    weight_sum = weight_sum * factor + jnp.sum(weights, axis=2)
    weighted = weighted * factor[:, :, None] + jnp.einsum(
        "qhk,khd->qhd", weights.astype(jnp.bfloat16), value_part, preferred_element_type=jnp.float32
    )
    return (new_max, weight_sum, weighted)


def maybe_fold(carry_state, query_heads, query_segs, keyval, key_segs, local_cols, score_scale):
    return fold_keys(
        carry_state, query_heads, query_segs, keyval, key_segs, local_cols, score_scale
    )


def per_device(
    tokens,
    segment_ids,
    ln_att_gain,
    w_query,
    w_keyval,
    w_out,
    ln_conv_gain,
    w_glu,
    w_depth,
    bn_scale,
    bn_shift,
    w_proj,
):
    row_count = tokens.shape[0]
    full_width = ln_att_gain.shape[0]
    local_cols = w_query.shape[1]
    heads_here = local_cols // HEAD_DIM
    score_scale = HEAD_DIM ** (-0.5)
    all_segs = lax.all_gather(segment_ids, "tm", axis=0, tiled=True)
    anchor = lax.axis_index("tm") * row_count
    whole_rows = lax.all_gather(tokens, "mp", axis=1, tiled=True)
    normed = layer_norm(whole_rows.astype(jnp.float32), ln_att_gain).astype(jnp.bfloat16)
    queries = jnp.dot(normed, w_query, preferred_element_type=jnp.float32).astype(jnp.bfloat16)
    keyval = jnp.dot(
        normed, w_keyval.reshape(full_width, -1), preferred_element_type=jnp.float32
    ).astype(jnp.bfloat16)
    query_heads = queries.reshape(row_count, heads_here, HEAD_DIM)
    initial = (
        jnp.full((row_count, heads_here), -jnp.inf, jnp.float32),
        jnp.zeros((row_count, heads_here), jnp.float32),
        jnp.zeros((row_count, heads_here, HEAD_DIM), jnp.float32),
    )
    segment = lax.all_gather(keyval, "tm", axis=0, tiled=True)
    piece_rows = segment.shape[0]
    block_count = piece_rows // row_count

    def inner_step(state_in, element):
        return (
            maybe_fold(
                state_in, query_heads, segment_ids, element[0], element[1], local_cols, score_scale
            ),
            None,
        )

    stacked = (
        segment.reshape(block_count, row_count, -1),
        all_segs.reshape(block_count, row_count),
    )
    result, unused = lax.scan(inner_step, initial, stacked)
    row_max, weight_sum, weighted = result
    context = (
        (weighted / weight_sum[:, :, None]).reshape(row_count, local_cols).astype(jnp.bfloat16)
    )
    att_terms = jnp.dot(context, w_out, preferred_element_type=jnp.float32)
    att_summed = lax.psum_scatter(
        att_terms.astype(jnp.bfloat16), "mp", scatter_dimension=1, tiled=True
    ).astype(jnp.float32)
    middle = (tokens.astype(jnp.float32) + att_summed).astype(jnp.bfloat16)
    whole_mid = lax.all_gather(middle, "mp", axis=1, tiled=True)
    normed_conv = layer_norm(whole_mid.astype(jnp.float32), ln_conv_gain).astype(jnp.bfloat16)
    both_halves = jnp.dot(
        normed_conv, w_glu.reshape(full_width, -1), preferred_element_type=jnp.float32
    )
    gated = (both_halves[:, :local_cols] * jax.nn.sigmoid(both_halves[:, local_cols:])).astype(
        jnp.bfloat16
    )
    half_width = (w_depth.shape[0] - 1) // 2
    extended = with_halo(gated, (("tm", 0),), half_width).astype(jnp.float32)
    padded_segs = jnp.pad(all_segs, (half_width, half_width), constant_values=-1)
    window_segs = lax.dynamic_slice_in_dim(padded_segs, anchor, row_count + 2 * half_width, 0)
    depth = jnp.zeros((row_count, local_cols), jnp.float32)
    for tap_index in range(w_depth.shape[0]):
        same_seg = (window_segs[tap_index : tap_index + row_count] == segment_ids)[:, None]
        shifted = jnp.where(same_seg, extended[tap_index : tap_index + row_count], 0.0)
        depth = depth + shifted * w_depth[tap_index].astype(jnp.float32)
    normalized = depth * bn_scale + bn_shift
    swished = (normalized * jax.nn.sigmoid(normalized)).astype(jnp.bfloat16)
    conv_terms = jnp.dot(swished, w_proj, preferred_element_type=jnp.float32)
    conv_summed = lax.psum_scatter(
        conv_terms.astype(jnp.bfloat16), "mp", scatter_dimension=1, tiled=True
    ).astype(jnp.float32)
    return (middle.astype(jnp.float32) + conv_summed).astype(jnp.bfloat16)


NEG = -1e30
HALO = 16
NCH = 2
MESH = pl.DeviceIdType.MESH
F32 = jnp.float32
BF16 = jnp.bfloat16


def block_kernel(
    T, taps,
    tokens, segrow, segcol, g_att, wq_h, wkv_h, wo_h, g_conv, wg_h, wdep, bns, bnb, wp_h,
    out,
    tok, seg_all, seg_ext, wq, wkv, wo, wg, wp, nrm, kbuf, qm, vm, sc, pw, mst, lst, acc,
    ctx, keep, mid, ext, wdf, sa, sx, sb, ra, rx, rb,
    wsem, tok_recv, z_send, x_send, m_send, seg_send, seg_recv, hs_send, hs_recv,
    hg_send, hg_recv, rs_send, rs_recv, mid_send, mid_recv,
):
    R, C = tokens.shape
    M = 4
    D = M * C
    heads = C // HEAD_DIM
    CR = R // NCH
    t = lax.axis_index("tm")
    m = lax.axis_index("mp")
    mate = m + 1 - 2 * (m % 2)
    cross = (m + 2) % 4
    diag = (mate + 2) % 4

    def rcopy(src, dst, ssem, rsem, **dev):
        return pltpu.make_async_remote_copy(
            src_ref=src, dst_ref=dst, send_sem=ssem, recv_sem=rsem,
            device_id=dev, device_id_type=MESH,
        )

    loads = [
        pltpu.make_async_copy(wq_h, wq, wsem.at[0]),
        pltpu.make_async_copy(wkv_h, wkv, wsem.at[1]),
        pltpu.make_async_copy(wg_h, wg, wsem.at[2]),
    ]
    for b in range(M):
        cols = pl.ds(b * C, C)
        loads.append(pltpu.make_async_copy(wo_h.at[:, cols], wo.at[b], wsem.at[3 + b]))
        loads.append(pltpu.make_async_copy(wp_h.at[:, cols], wp.at[b], wsem.at[7 + b]))
    for c in loads:
        c.start()

    barrier = pltpu.get_barrier_semaphore()
    for peer in (mate, cross):
        pl.semaphore_signal(barrier, inc=1, device_id={"mp": peer}, device_id_type=MESH)
    for d in range(1, T):
        pl.semaphore_signal(
            barrier, inc=1, device_id={"tm": (t + d) % T}, device_id_type=MESH
        )
    tok[t, m] = tokens[...]
    seg_all[t] = segrow[...]
    seg_ext[0, pl.ds(HALO, R), :] = segcol[...]
    pl.semaphore_wait(barrier, 1 + T)

    def z_right(s):
        return rcopy(tok.at[s, m], tok.at[s, m], z_send.at[0, s], tok_recv.at[s, m],
                     tm=(t + 1) % T)

    def z_left(s):
        return rcopy(tok.at[s, m], tok.at[s, m], z_send.at[1, s], tok_recv.at[s, m],
                     tm=(t + T - 1) % T)

    def over_x(s, col):
        return rcopy(tok.at[s, col], tok.at[s, col], x_send.at[s], tok_recv.at[s, col],
                     mp=cross)

    def to_mate(s, col, k):
        return rcopy(tok.at[s, col], tok.at[s, col], m_send.at[s, k], tok_recv.at[s, col],
                     mp=mate)

    def launch(s):
        @pl.when(jnp.logical_and(s <= t, t < T - 1))
        def _():
            z_right(s).start()

        @pl.when(jnp.logical_and(s >= t, t > 0))
        def _():
            z_left(s).start()

        over_x(s, m).start()
        to_mate(s, m, 0).start()

    launch(t)

    def seg_copy(d):
        return rcopy(seg_all.at[t], seg_all.at[t], seg_send.at[d], seg_recv.at[t],
                     tm=(t + d) % T)

    for d in range(1, T):
        seg_copy(d).start()

    def halo_right(ref, ssem, rsem):
        return rcopy(ref.at[:, pl.ds(R, HALO)], ref.at[:, pl.ds(0, HALO)], ssem.at[0],
                     rsem.at[0], tm=(t + 1) % T)

    def halo_left(ref, ssem, rsem):
        return rcopy(ref.at[:, pl.ds(HALO, HALO)], ref.at[:, pl.ds(R + HALO, HALO)],
                     ssem.at[1], rsem.at[1], tm=(t + T - 1) % T)

    has_right = t < T - 1
    has_left = t > 0

    @pl.when(has_right)
    def _():
        halo_right(seg_ext, hs_send, hs_recv).start()

    @pl.when(has_left)
    def _():
        halo_left(seg_ext, hs_send, hs_recv).start()

    @pl.when(jnp.logical_not(has_left))
    def _():
        seg_ext[0, pl.ds(0, HALO), :] = jnp.full((HALO, 128), -1, jnp.int32)
        ext[:, pl.ds(0, HALO), :] = jnp.zeros((C // 128, HALO, 128), F32)

    @pl.when(jnp.logical_not(has_right))
    def _():
        seg_ext[0, pl.ds(R + HALO, HALO), :] = jnp.full((HALO, 128), -1, jnp.int32)
        ext[:, pl.ds(R + HALO, HALO), :] = jnp.zeros((C // 128, HALO, 128), F32)

    wdf[pl.ds(0, taps), :] = wdep[...].astype(F32)
    mst[...] = jnp.full(mst.shape, NEG, F32)
    lst[...] = jnp.zeros(lst.shape, F32)
    acc[...] = jnp.zeros(acc.shape, F32)
    head_of = lax.broadcasted_iota(jnp.int32, (1, C), 1) // HEAD_DIM

    def norm_rows(load, gain, r0, n):
        parts = [load(b, r0, n).astype(F32) for b in range(M)]
        total = parts[0] + parts[1] + parts[2] + parts[3]
        mean = jnp.sum(total, axis=1, keepdims=True) * (1.0 / D)
        parts = [p - mean for p in parts]
        sq = parts[0] * parts[0]
        for p in parts[1:]:
            sq = sq + p * p
        inv = lax.rsqrt(jnp.sum(sq, axis=1, keepdims=True) * (1.0 / D) + 1e-05)
        for b in range(M):
            nrm[pl.ds(r0, n), pl.ds(b * C, C)] = (
                parts[b] * inv * gain[:, pl.ds(b * C, C)]
            ).astype(BF16)

    RT = 32
    coef = float(HEAD_DIM ** (-0.5) * 1.4426950408889634)

    def softmax_rows(s, rt):
        r0 = pl.multiple_of(rt * RT, RT)
        rows = pl.ds(r0, RT)
        same = segcol[rows, pl.ds(0, 1)] == seg_all[s, pl.ds(0, 1), :]
        bias = jnp.where(same, 0.0, NEG)
        lanes = None
        for h in range(heads):
            x = sc[pl.ds(pl.multiple_of(h * R + r0, RT), RT), :] + bias
            old = mst[h, rows, :]
            new = jnp.maximum(old, jnp.max(x, axis=1, keepdims=True))
            f = jnp.exp2((old - new) * coef)
            p = jnp.exp2((x - new[:, :1]) * coef)
            lst[h, rows, :] = lst[h, rows, :] * f + jnp.sum(p, axis=1, keepdims=True)
            mst[h, rows, :] = new
            pw[rows, pl.ds(h * R, R)] = p.astype(BF16)
            wide = jnp.broadcast_to(f[:, :1], (RT, C))
            lanes = wide if lanes is None else jnp.where(head_of == h, wide, lanes)
        acc[rows, :] = acc[rows, :] * lanes

    def block_step(i, code):
        s = code % T
        nxt = (code // T) % T

        @pl.when(i + 1 < T)
        def _():
            z_right(nxt).wait_recv()
            launch(nxt)

        over_x(s, cross).wait_recv()
        to_mate(s, cross, 1).start()
        to_mate(s, mate, 0).wait_recv()
        to_mate(s, diag, 1).wait_recv()

        @pl.when(i == 0)
        def _():
            loads[0].wait()
            loads[1].wait()

        @pl.when(i > 0)
        def _():
            rcopy(seg_all.at[s], seg_all.at[s], seg_send.at[0], seg_recv.at[s],
                  tm=(t + 1) % T).wait_recv()

        @pl.loop(0, R // RT)
        def _(rt):
            norm_rows(lambda b, r0, n: tok[s, b, pl.ds(r0, n), :], g_att,
                      pl.multiple_of(rt * RT, RT), RT)

        @pl.when(i == 0)
        def _():
            q = jnp.dot(nrm[...], wq[...], preferred_element_type=F32).astype(BF16)
            for h in range(heads):
                qm[pl.ds(h * R, R), :] = jnp.where(head_of == h, q, jnp.zeros_like(q))

        kbuf[...] = jnp.dot(
            nrm[...], wkv[:, pl.ds(0, C)], preferred_element_type=F32).astype(BF16)
        v = jnp.dot(nrm[...], wkv[:, pl.ds(C, C)], preferred_element_type=F32).astype(BF16)
        for h in range(heads):
            vm[pl.ds(h * R, R), :] = jnp.where(head_of == h, v, jnp.zeros_like(v))
        for h in range(heads):
            sc[pl.ds(h * R, R), :] = lax.dot_general(
                qm[pl.ds(h * R, R), :], kbuf[...], (((1,), (1,)), ((), ())),
                preferred_element_type=F32)

        @pl.loop(0, R // RT)
        def _(rt):
            softmax_rows(s, rt)

        acc[...] += jnp.dot(pw[...], vm[...], preferred_element_type=F32)
        return code // T

    order = 228 - 3 * ((t + 3) // 4) - 171 * ((t + 2) // 4) - 27 * ((t + 1) // 4)
    lax.fori_loop(0, T, block_step, order)

    den = None
    for h in range(heads):
        wide = jnp.broadcast_to(lst[h, :, pl.ds(0, 1)], (R, C))
        den = wide if den is None else jnp.where(head_of == h, wide, den)
    ctx[...] = (acc[...] / den).astype(BF16)

    def rs_a(ph, ch):
        return rcopy(sa.at[ph, ch], ra.at[ph, ch], rs_send.at[ph, ch, 0],
                     rs_recv.at[ph, ch, 0], mp=mate)

    def rs_x(ph, ch):
        return rcopy(sx.at[ph, ch], rx.at[ph, ch], rs_send.at[ph, ch, 1],
                     rs_recv.at[ph, ch, 1], mp=cross)

    def rs_b(ph, ch):
        return rcopy(sb.at[ph, ch], rb.at[ph, ch], rs_send.at[ph, ch, 2],
                     rs_recv.at[ph, ch, 2], mp=mate)

    def scatter_chunk(ph, w, ch):
        a = ctx[pl.ds(ch * CR, CR), :]
        sa[ph, ch] = jnp.dot(a, w[diag], preferred_element_type=F32).astype(BF16)
        rs_a(ph, ch).start()
        mine = jnp.dot(a, w[cross], preferred_element_type=F32)
        sb[ph, ch] = jnp.dot(a, w[mate], preferred_element_type=F32).astype(BF16)
        rs_b(ph, ch).start()
        rs_a(ph, ch).wait_recv()
        sx[ph, ch] = (mine + ra[ph, ch].astype(F32)).astype(BF16)
        rs_x(ph, ch).start()
        keep[pl.ds(ch * CR, CR), :] = (
            jnp.dot(a, w[m], preferred_element_type=F32).astype(BF16).astype(F32))

    def summed(ph, ch):
        rs_b(ph, ch).wait_recv()
        rs_x(ph, ch).wait_recv()
        return (keep[pl.ds(ch * CR, CR), :] + rb[ph, ch].astype(F32)) + rx[ph, ch].astype(F32)

    for b in range(M):
        loads[3 + 2 * b].wait()
    for ch in range(NCH):
        scatter_chunk(0, wo, ch)

    def mid_copy(col, ch, k, **dev):
        piece = mid.at[col, pl.ds(ch * CR, CR)]
        return rcopy(piece, piece, mid_send.at[ch, k], mid_recv.at[col, ch], **dev)

    for ch in range(NCH):
        rows = pl.ds(ch * CR, CR)
        mid[m, rows, :] = (tokens[rows, :].astype(F32) + summed(0, ch)).astype(BF16)
        mid_copy(m, ch, 0, mp=cross).start()
        mid_copy(m, ch, 1, mp=mate).start()
    loads[2].wait()
    for ch in range(NCH):
        rows = pl.ds(ch * CR, CR)
        mid_copy(cross, ch, 0, mp=cross).wait_recv()
        mid_copy(cross, ch, 2, mp=mate).start()
        mid_copy(mate, ch, 1, mp=mate).wait_recv()
        mid_copy(diag, ch, 2, mp=mate).wait_recv()

        @pl.loop(0, CR // RT)
        def _(rt):
            norm_rows(lambda b, r0, n: mid[b, pl.ds(r0, n), :], g_conv,
                      pl.multiple_of(ch * CR + rt * RT, RT), RT)

        a = nrm[rows, :]
        val = jnp.dot(a, wg[:, pl.ds(0, C)], preferred_element_type=F32)
        gate = jnp.dot(a, wg[:, pl.ds(C, C)], preferred_element_type=F32)
        gated = (val * jax.nn.sigmoid(gate)).astype(BF16).astype(F32)
        for k in range(C // 128):
            ext[k, pl.ds(HALO + ch * CR, CR), :] = gated[:, k * 128:(k + 1) * 128]
        if ch == 0:
            @pl.when(has_left)
            def _():
                halo_left(ext, hg_send, hg_recv).start()

    @pl.when(has_right)
    def _():
        halo_right(ext, hg_send, hg_recv).start()

    @pl.when(has_left)
    def _():
        halo_right(seg_ext, hs_send, hs_recv).wait_recv()
        halo_right(ext, hg_send, hg_recv).wait_recv()

    @pl.when(has_right)
    def _():
        halo_left(seg_ext, hs_send, hs_recv).wait_recv()
        halo_left(ext, hg_send, hg_recv).wait_recv()

    half = (taps - 1) // 2
    for b in range(M):
        loads[4 + 2 * b].wait()
    for ch in range(NCH):
        @pl.loop(0, CR // RT)
        def _(rt):
            r0 = pl.multiple_of(ch * CR + rt * RT, RT)
            here = segcol[pl.ds(r0, RT), :]
            groups = [pl.ds(k * 128, 128) for k in range(C // 128)]
            depth = [jnp.zeros((RT, 128), F32) for _ in groups]
            for j in range(taps):
                at = pl.ds(r0 + (j + HALO - half), RT)
                same = seg_ext[0, at, :] == here
                for k, g in enumerate(groups):
                    depth[k] += jnp.where(same, ext[k, at, :], 0.0) * wdf[pl.ds(j, 1), g]
            for k, g in enumerate(groups):
                z = depth[k] * bns[:, g] + bnb[:, g]
                ctx[pl.ds(r0, RT), g] = (z * jax.nn.sigmoid(z)).astype(BF16)

        scatter_chunk(1, wp, ch)
    for ch in range(NCH):
        rows = pl.ds(ch * CR, CR)
        out[rows, :] = (mid[m, rows, :].astype(F32) + summed(1, ch)).astype(BF16)

    for s in range(T):
        @pl.when(jnp.logical_and(s <= t, t < T - 1))
        def _():
            z_right(s).wait_send()

        @pl.when(jnp.logical_and(s >= t, t > 0))
        def _():
            z_left(s).wait_send()

        over_x(s, m).wait_send()
        to_mate(s, m, 0).wait_send()
        to_mate(s, cross, 1).wait_send()
    for d in range(1, T):
        seg_copy(d).wait_send()

    @pl.when(has_right)
    def _():
        halo_right(seg_ext, hs_send, hs_recv).wait_send()
        halo_right(ext, hg_send, hg_recv).wait_send()

    @pl.when(has_left)
    def _():
        halo_left(seg_ext, hs_send, hs_recv).wait_send()
        halo_left(ext, hg_send, hg_recv).wait_send()

    for ch in range(NCH):
        for ph in range(2):
            rs_a(ph, ch).wait_send()
            rs_x(ph, ch).wait_send()
            rs_b(ph, ch).wait_send()
        mid_copy(m, ch, 0, mp=cross).wait_send()
        mid_copy(m, ch, 1, mp=mate).wait_send()
        mid_copy(cross, ch, 2, mp=mate).wait_send()


def fused_device(
    tokens, segment_ids, ln_att_gain, w_query, w_keyval, w_out, ln_conv_gain, w_glu,
    w_depth, bn_scale, bn_shift, w_proj,
):
    R, C = tokens.shape
    D = ln_att_gain.shape[0]
    T = lax.axis_size("tm")
    M = D // C
    heads = C // HEAD_DIM
    taps = w_depth.shape[0]
    CR = R // NCH
    segrow = jnp.broadcast_to(segment_ids[None, :], (8, R))
    segcol = jnp.broadcast_to(segment_ids[:, None], (R, 128))
    vmem = pl.BlockSpec(memory_space=pltpu.VMEM)
    hbm = pl.BlockSpec(memory_space=pl.ANY)
    dma = pltpu.SemaphoreType.DMA
    part = pltpu.VMEM((2, NCH, CR, C), BF16)
    return pl.pallas_call(
        functools.partial(block_kernel, T, taps),
        out_shape=jax.ShapeDtypeStruct((R, C), BF16),
        in_specs=[vmem, vmem, vmem, vmem, hbm, hbm, hbm, vmem, hbm, vmem, vmem, vmem, hbm],
        out_specs=vmem,
        scratch_shapes=[
            pltpu.VMEM((T, M, R, C), BF16),
            pltpu.VMEM((T, 8, R), jnp.int32),
            pltpu.VMEM((1, R + 2 * HALO, 128), jnp.int32),
            pltpu.VMEM((D, C), BF16),
            pltpu.VMEM((D, 2 * C), BF16),
            pltpu.VMEM((M, C, C), BF16),
            pltpu.VMEM((D, 2 * C), BF16),
            pltpu.VMEM((M, C, C), BF16),
            pltpu.VMEM((R, D), BF16),
            pltpu.VMEM((R, C), BF16),
            pltpu.VMEM((heads * R, C), BF16),
            pltpu.VMEM((heads * R, C), BF16),
            pltpu.VMEM((heads * R, R), F32),
            pltpu.VMEM((R, heads * R), BF16),
            pltpu.VMEM((heads, R, 128), F32),
            pltpu.VMEM((heads, R, 128), F32),
            pltpu.VMEM((R, C), F32),
            pltpu.VMEM((R, C), BF16),
            pltpu.VMEM((R, C), F32),
            pltpu.VMEM((M, R, C), BF16),
            pltpu.VMEM((C // 128, R + 2 * HALO, 128), F32),
            pltpu.VMEM((32, C), F32),
            part, part, part, part, part, part,
            dma((11,)),
            dma((T, M)), dma((2, T)), dma((T,)), dma((T, 2)),
            dma((T,)), dma((T,)), dma((2,)), dma((2,)), dma((2,)), dma((2,)),
            dma((2, NCH, 3)), dma((2, NCH, 3)), dma((NCH, 3)), dma((M, NCH)),
        ],
        compiler_params=pltpu.CompilerParams(
            collective_id=0, has_side_effects=True, vmem_limit_bytes=52 * 2**20
        ),
    )(
        tokens, segrow, segcol, ln_att_gain[None, :], w_query, w_keyval.reshape(D, 2 * C),
        w_out, ln_conv_gain[None, :], w_glu.reshape(D, 2 * C), w_depth, bn_scale[None, :],
        bn_shift[None, :], w_proj,
    )


def solution(mesh):
    placed = (
        P(("group", "tm"), "mp"),
        P(("group", "tm")),
        P(),
        P(None, "mp"),
        P(None, None, "mp"),
        P("mp", None),
        P(),
        P(None, None, "mp"),
        P(None, "mp"),
        P("mp"),
        P("mp"),
        P("mp", None),
    )
    fused = mesh.shape["tm"] == 4 and mesh.shape["mp"] == 4
    return jax.shard_map(
        fused_device if fused else per_device, mesh=mesh, in_specs=placed, out_specs=P(("group", "tm"), "mp"), check_vma=False
    )
```

```python
import functools

import jax
import jax.numpy as jnp
from jax import lax
from jax.experimental import pallas as pl
from jax.experimental.pallas import tpu as pltpu
from jax.sharding import PartitionSpec as P

HEAD_DIM = 96


def with_halo(value, sides, width):
    for axis, dim in sides:
        count, length = (lax.axis_size(axis), value.shape[dim])
        up = [(i, (i + 1) % count) for i in range(count - 1)]
        down = [(j, i) for i, j in up]
        last = lax.slice_in_dim(value, length - width, length, axis=dim)
        initial = lax.slice_in_dim(value, 0, width, axis=dim)
        before = lax.ppermute(last, axis, up)
        after = lax.ppermute(initial, axis, down)
        value = jnp.concatenate([before, value, after], axis=dim)
    return value


def layer_norm(values_in, gain_vec):
    row_mean = jnp.mean(values_in, axis=-1, keepdims=True)
    centered = values_in - row_mean
    spread = jnp.mean(centered * centered, axis=-1, keepdims=True)
    return centered * lax.rsqrt(spread + 1e-05) * gain_vec


def fold_keys(carry_state, query_heads, query_segs, keyval, key_segs, local_cols, score_scale):
    row_max, weight_sum, weighted = carry_state
    key_rows = keyval.shape[0]
    heads_here = query_heads.shape[1]
    key_part = keyval[:, :local_cols].reshape(key_rows, heads_here, -1)
    value_part = keyval[:, local_cols:].reshape(key_rows, heads_here, -1)
    scores = (
        jnp.einsum("qhd,khd->qhk", query_heads, key_part, preferred_element_type=jnp.float32)
        * score_scale
    )
    same_seg = (query_segs[:, None] == key_segs[None, :])[:, None, :]
    scores = jnp.where(same_seg, scores, -jnp.inf)
    new_max = jnp.maximum(row_max, jnp.max(scores, axis=2))
    safe_max = jnp.where(new_max == -jnp.inf, 0.0, new_max)
    weights = jnp.exp(scores - safe_max[:, :, None])
    factor = jnp.exp(row_max - safe_max)
    weight_sum = weight_sum * factor + jnp.sum(weights, axis=2)
    weighted = weighted * factor[:, :, None] + jnp.einsum(
        "qhk,khd->qhd", weights.astype(jnp.bfloat16), value_part, preferred_element_type=jnp.float32
    )
    return (new_max, weight_sum, weighted)


def maybe_fold(carry_state, query_heads, query_segs, keyval, key_segs, local_cols, score_scale):
    return fold_keys(
        carry_state, query_heads, query_segs, keyval, key_segs, local_cols, score_scale
    )


def per_device(
    tokens,
    segment_ids,
    ln_att_gain,
    w_query,
    w_keyval,
    w_out,
    ln_conv_gain,
    w_glu,
    w_depth,
    bn_scale,
    bn_shift,
    w_proj,
):
    row_count = tokens.shape[0]
    full_width = ln_att_gain.shape[0]
    local_cols = w_query.shape[1]
    heads_here = local_cols // HEAD_DIM
    score_scale = HEAD_DIM ** (-0.5)
    all_segs = lax.all_gather(segment_ids, "tm", axis=0, tiled=True)
    anchor = lax.axis_index("tm") * row_count
    whole_rows = lax.all_gather(tokens, "mp", axis=1, tiled=True)
    normed = layer_norm(whole_rows.astype(jnp.float32), ln_att_gain).astype(jnp.bfloat16)
    queries = jnp.dot(normed, w_query, preferred_element_type=jnp.float32).astype(jnp.bfloat16)
    keyval = jnp.dot(
        normed, w_keyval.reshape(full_width, -1), preferred_element_type=jnp.float32
    ).astype(jnp.bfloat16)
    query_heads = queries.reshape(row_count, heads_here, HEAD_DIM)
    initial = (
        jnp.full((row_count, heads_here), -jnp.inf, jnp.float32),
        jnp.zeros((row_count, heads_here), jnp.float32),
        jnp.zeros((row_count, heads_here, HEAD_DIM), jnp.float32),
    )
    segment = lax.all_gather(keyval, "tm", axis=0, tiled=True)
    piece_rows = segment.shape[0]
    block_count = piece_rows // row_count

    def inner_step(state_in, element):
        return (
            maybe_fold(
                state_in, query_heads, segment_ids, element[0], element[1], local_cols, score_scale
            ),
            None,
        )

    stacked = (
        segment.reshape(block_count, row_count, -1),
        all_segs.reshape(block_count, row_count),
    )
    result, unused = lax.scan(inner_step, initial, stacked)
    row_max, weight_sum, weighted = result
    context = (
        (weighted / weight_sum[:, :, None]).reshape(row_count, local_cols).astype(jnp.bfloat16)
    )
    att_terms = jnp.dot(context, w_out, preferred_element_type=jnp.float32)
    att_summed = lax.psum_scatter(
        att_terms.astype(jnp.bfloat16), "mp", scatter_dimension=1, tiled=True
    ).astype(jnp.float32)
    middle = (tokens.astype(jnp.float32) + att_summed).astype(jnp.bfloat16)
    whole_mid = lax.all_gather(middle, "mp", axis=1, tiled=True)
    normed_conv = layer_norm(whole_mid.astype(jnp.float32), ln_conv_gain).astype(jnp.bfloat16)
    both_halves = jnp.dot(
        normed_conv, w_glu.reshape(full_width, -1), preferred_element_type=jnp.float32
    )
    gated = (both_halves[:, :local_cols] * jax.nn.sigmoid(both_halves[:, local_cols:])).astype(
        jnp.bfloat16
    )
    half_width = (w_depth.shape[0] - 1) // 2
    extended = with_halo(gated, (("tm", 0),), half_width).astype(jnp.float32)
    padded_segs = jnp.pad(all_segs, (half_width, half_width), constant_values=-1)
    window_segs = lax.dynamic_slice_in_dim(padded_segs, anchor, row_count + 2 * half_width, 0)
    depth = jnp.zeros((row_count, local_cols), jnp.float32)
    for tap_index in range(w_depth.shape[0]):
        same_seg = (window_segs[tap_index : tap_index + row_count] == segment_ids)[:, None]
        shifted = jnp.where(same_seg, extended[tap_index : tap_index + row_count], 0.0)
        depth = depth + shifted * w_depth[tap_index].astype(jnp.float32)
    normalized = depth * bn_scale + bn_shift
    swished = (normalized * jax.nn.sigmoid(normalized)).astype(jnp.bfloat16)
    conv_terms = jnp.dot(swished, w_proj, preferred_element_type=jnp.float32)
    conv_summed = lax.psum_scatter(
        conv_terms.astype(jnp.bfloat16), "mp", scatter_dimension=1, tiled=True
    ).astype(jnp.float32)
    return (middle.astype(jnp.float32) + conv_summed).astype(jnp.bfloat16)


NEG = -1e30
HALO = 16
NCH = 2
MESH = pl.DeviceIdType.MESH
F32 = jnp.float32
BF16 = jnp.bfloat16


def block_kernel(
    T, taps,
    tokens, seg, g_att, wq_h, wkv_h, wo_h, g_conv, wg_h, wdep, bn_s, bn_b, wp_h,
    out, segcol, gains, bns, bnb,
    tok, seg_all, seg_ext, wq, wkv, wo, wg, wp, nrm, kbuf, qm, vm, sc, pw, mst, lst, acc,
    ctx, keep, mid, ext, wdf, sa, sx, sb, ra, rx, rb,
    wsem, tok_recv, z_send, x_send, m_send, seg_send, seg_recv, hs_send, hs_recv,
    hg_send, hg_recv, rs_send, rs_recv, mid_send, mid_recv,
):
    R, C = tokens.shape
    M = 4
    D = M * C
    heads = C // HEAD_DIM
    CR = R // NCH
    t = lax.axis_index("tm")
    m = lax.axis_index("mp")
    mate = m + 1 - 2 * (m % 2)
    cross = (m + 2) % 4
    diag = (mate + 2) % 4

    def rcopy(src, dst, ssem, rsem, **dev):
        return pltpu.make_async_remote_copy(
            src_ref=src, dst_ref=dst, send_sem=ssem, recv_sem=rsem,
            device_id=dev, device_id_type=MESH,
        )

    loads = [
        pltpu.make_async_copy(wq_h, wq, wsem.at[0]),
        pltpu.make_async_copy(wkv_h, wkv, wsem.at[1]),
        pltpu.make_async_copy(wg_h, wg, wsem.at[2]),
    ]
    for b in range(M):
        cols = pl.ds(b * C, C)
        loads.append(pltpu.make_async_copy(wo_h.at[:, cols], wo.at[b], wsem.at[3 + b]))
        loads.append(pltpu.make_async_copy(wp_h.at[:, cols], wp.at[b], wsem.at[7 + b]))
    for c in loads:
        c.start()

    barrier = pltpu.get_barrier_semaphore()
    for peer in (mate, cross):
        pl.semaphore_signal(barrier, inc=1, device_id={"mp": peer}, device_id_type=MESH)
    for d in range(1, T):
        pl.semaphore_signal(
            barrier, inc=1, device_id={"tm": (t + d) % T}, device_id_type=MESH
        )
    tok[t, m] = tokens[...]
    ids = seg[...].reshape(1, R)
    seg_all[t] = jnp.broadcast_to(ids, (8, R))
    segcol[...] = jnp.transpose(jnp.broadcast_to(ids, (128, R)))
    seg_ext[0, pl.ds(HALO, R), :] = segcol[...]
    gains[0] = g_att[...].reshape(1, D)
    gains[1] = g_conv[...].reshape(1, D)
    bns[...] = bn_s[...].reshape(1, C)
    bnb[...] = bn_b[...].reshape(1, C)
    pl.semaphore_wait(barrier, 1 + T)

    def z_right(s):
        return rcopy(tok.at[s, m], tok.at[s, m], z_send.at[0, s], tok_recv.at[s, m],
                     tm=(t + 1) % T)

    def z_left(s):
        return rcopy(tok.at[s, m], tok.at[s, m], z_send.at[1, s], tok_recv.at[s, m],
                     tm=(t + T - 1) % T)

    def over_x(s, col):
        return rcopy(tok.at[s, col], tok.at[s, col], x_send.at[s], tok_recv.at[s, col],
                     mp=cross)

    def to_mate(s, col, k):
        return rcopy(tok.at[s, col], tok.at[s, col], m_send.at[s, k], tok_recv.at[s, col],
                     mp=mate)

    def launch(s):
        @pl.when(jnp.logical_and(s <= t, t < T - 1))
        def _():
            z_right(s).start()

        @pl.when(jnp.logical_and(s >= t, t > 0))
        def _():
            z_left(s).start()

        to_mate(s, m, 0).start()

    launch(t)
    over_x(t, m).start()

    def seg_copy(d):
        return rcopy(seg_all.at[t], seg_all.at[t], seg_send.at[d], seg_recv.at[t],
                     tm=(t + d) % T)

    for d in range(1, T):
        seg_copy(d).start()

    def halo_right(ref, ssem, rsem):
        return rcopy(ref.at[:, pl.ds(R, HALO)], ref.at[:, pl.ds(0, HALO)], ssem.at[0],
                     rsem.at[0], tm=(t + 1) % T)

    def halo_left(ref, ssem, rsem):
        return rcopy(ref.at[:, pl.ds(HALO, HALO)], ref.at[:, pl.ds(R + HALO, HALO)],
                     ssem.at[1], rsem.at[1], tm=(t + T - 1) % T)

    has_right = t < T - 1
    has_left = t > 0
    edge = jnp.logical_or(t == 0, t == T - 1)

    @pl.when(has_right)
    def _():
        halo_right(seg_ext, hs_send, hs_recv).start()

    @pl.when(has_left)
    def _():
        halo_left(seg_ext, hs_send, hs_recv).start()

    @pl.when(jnp.logical_not(has_left))
    def _():
        seg_ext[0, pl.ds(0, HALO), :] = jnp.full((HALO, 128), -1, jnp.int32)
        ext[:, pl.ds(0, HALO), :] = jnp.zeros((C // 128, HALO, 128), F32)

    @pl.when(jnp.logical_not(has_right))
    def _():
        seg_ext[0, pl.ds(R + HALO, HALO), :] = jnp.full((HALO, 128), -1, jnp.int32)
        ext[:, pl.ds(R + HALO, HALO), :] = jnp.zeros((C // 128, HALO, 128), F32)

    wdf[pl.ds(0, taps), :] = wdep[...].astype(F32)
    mst[...] = jnp.full(mst.shape, NEG, F32)
    lst[...] = jnp.zeros(lst.shape, F32)
    acc[...] = jnp.zeros(acc.shape, F32)
    head_of = lax.broadcasted_iota(jnp.int32, (1, C), 1) // HEAD_DIM

    def norm_rows(load, gain, r0, n):
        parts = [load(b, r0, n).astype(F32) for b in range(M)]
        total = parts[0] + parts[1] + parts[2] + parts[3]
        mean = jnp.sum(total, axis=1, keepdims=True) * (1.0 / D)
        parts = [p - mean for p in parts]
        sq = parts[0] * parts[0]
        for p in parts[1:]:
            sq = sq + p * p
        inv = lax.rsqrt(jnp.sum(sq, axis=1, keepdims=True) * (1.0 / D) + 1e-05)
        for b in range(M):
            nrm[pl.ds(r0, n), pl.ds(b * C, C)] = (
                parts[b] * inv * gains[gain, :, pl.ds(b * C, C)]
            ).astype(BF16)

    RT = 32
    coef = float(HEAD_DIM ** (-0.5))

    def wide(col):
        return jnp.concatenate([col] * (C // 128), axis=1)

    def softmax_rows(s, rt):
        r0 = pl.multiple_of(rt * RT, RT)
        rows = pl.ds(r0, RT)
        bias = jnp.where(wide(segcol[rows, :]) == seg_all[s, pl.ds(0, 1), :], 0.0, NEG)
        hs = range(heads)
        xs = [sc[pl.ds(pl.multiple_of(h * R + r0, RT), RT), :] + bias for h in hs]
        olds = [mst[h, rows, :] for h in hs]
        sums = [lst[h, rows, :] for h in hs]
        news = [jnp.maximum(o, jnp.max(x, axis=1, keepdims=True)) for o, x in zip(olds, xs)]
        fs = [jnp.exp((o - n) * coef) for o, n in zip(olds, news)]
        ps = [jnp.exp((x - wide(n)) * coef) for x, n in zip(xs, news)]
        sums = [v * f + jnp.sum(p, axis=1, keepdims=True) for v, f, p in zip(sums, fs, ps)]
        lanes = wide(fs[0])
        for h in hs[1:]:
            lanes = jnp.where(head_of == h, wide(fs[h]), lanes)
        for h in hs:
            mst[h, rows, :] = news[h]
            lst[h, rows, :] = sums[h]
            pw[rows, pl.ds(h * R, R)] = ps[h].astype(BF16)
        acc[rows, :] = acc[rows, :] * lanes

    def block_step(i, code):
        s = code % T
        nxt = (code // T) % T
        after = (code // (T * T)) % T

        @pl.when(jnp.logical_or(i == 0, jnp.logical_and(edge, i + 1 < T)))
        def _():
            z_right(nxt).wait_recv()
            launch(nxt)

        @pl.when(jnp.logical_and(jnp.logical_not(edge), i < 2))
        def _():
            z_right(after).wait_recv()
            launch(after)

        @pl.when(i + 1 < T)
        def _():
            over_x(nxt, m).start()

        over_x(s, cross).wait_recv()
        to_mate(s, cross, 1).start()
        to_mate(s, mate, 0).wait_recv()
        to_mate(s, diag, 1).wait_recv()

        @pl.when(i == 0)
        def _():
            loads[0].wait()
            loads[1].wait()

        @pl.when(i > 0)
        def _():
            rcopy(seg_all.at[s], seg_all.at[s], seg_send.at[0], seg_recv.at[s],
                  tm=(t + 1) % T).wait_recv()

        @pl.loop(0, R // RT)
        def _(rt):
            norm_rows(lambda b, r0, n: tok[s, b, pl.ds(r0, n), :], 0,
                      pl.multiple_of(rt * RT, RT), RT)

        @pl.when(i == 0)
        def _():
            q = jnp.dot(nrm[...], wq[...], preferred_element_type=F32).astype(BF16)
            for h in range(heads):
                qm[pl.ds(h * R, R), :] = jnp.where(head_of == h, q, jnp.zeros_like(q))

        kbuf[...] = jnp.dot(
            nrm[...], wkv[:, pl.ds(0, C)], preferred_element_type=F32).astype(BF16)
        v = jnp.dot(nrm[...], wkv[:, pl.ds(C, C)], preferred_element_type=F32).astype(BF16)
        for h in range(heads):
            vm[pl.ds(h * R, R), :] = jnp.where(head_of == h, v, jnp.zeros_like(v))
        for h in range(heads):
            sc[pl.ds(h * R, R), :] = lax.dot_general(
                qm[pl.ds(h * R, R), :], kbuf[...], (((1,), (1,)), ((), ())),
                preferred_element_type=F32)

        @pl.loop(0, R // RT)
        def _(rt):
            softmax_rows(s, rt)

        acc[...] += jnp.dot(pw[...], vm[...], preferred_element_type=F32)
        return code // T

    order = 228 - 3 * ((t + 3) // 4) - 171 * ((t + 2) // 4) - 27 * ((t + 1) // 4)
    lax.fori_loop(0, T, block_step, order)

    den = None
    for h in range(heads):
        col = wide(lst[h, :, :])
        den = col if den is None else jnp.where(head_of == h, col, den)
    ctx[...] = (acc[...] / den).astype(BF16)

    def rs_a(ph, ch):
        return rcopy(sa.at[ph, ch], ra.at[ph, ch], rs_send.at[ph, ch, 0],
                     rs_recv.at[ph, ch, 0], mp=mate)

    def rs_x(ph, ch):
        return rcopy(sx.at[ph, ch], rx.at[ph, ch], rs_send.at[ph, ch, 1],
                     rs_recv.at[ph, ch, 1], mp=cross)

    def rs_b(ph, ch):
        return rcopy(sb.at[ph, ch], rb.at[ph, ch], rs_send.at[ph, ch, 2],
                     rs_recv.at[ph, ch, 2], mp=mate)

    def scatter_chunk(ph, w, ch):
        a = ctx[pl.ds(ch * CR, CR), :]
        sa[ph, ch] = jnp.dot(a, w[diag], preferred_element_type=F32).astype(BF16)
        rs_a(ph, ch).start()
        mine = jnp.dot(a, w[cross], preferred_element_type=F32)
        sb[ph, ch] = jnp.dot(a, w[mate], preferred_element_type=F32).astype(BF16)
        rs_b(ph, ch).start()
        rs_a(ph, ch).wait_recv()
        sx[ph, ch] = (mine + ra[ph, ch].astype(F32)).astype(BF16)
        rs_x(ph, ch).start()
        keep[pl.ds(ch * CR, CR), :] = (
            jnp.dot(a, w[m], preferred_element_type=F32).astype(BF16).astype(F32))

    def summed(ph, ch):
        rs_b(ph, ch).wait_recv()
        rs_x(ph, ch).wait_recv()
        return (keep[pl.ds(ch * CR, CR), :] + rb[ph, ch].astype(F32)) + rx[ph, ch].astype(F32)

    for b in range(M):
        loads[3 + 2 * b].wait()
    for ch in range(NCH):
        scatter_chunk(0, wo, ch)

    def mid_copy(col, ch, k, **dev):
        piece = mid.at[col, pl.ds(ch * CR, CR)]
        return rcopy(piece, piece, mid_send.at[ch, k], mid_recv.at[col, ch], **dev)

    for ch in range(NCH):
        rows = pl.ds(ch * CR, CR)
        mid[m, rows, :] = (tokens[rows, :].astype(F32) + summed(0, ch)).astype(BF16)
        mid_copy(m, ch, 0, mp=cross).start()
        mid_copy(m, ch, 1, mp=mate).start()
    loads[2].wait()
    for ch in range(NCH):
        rows = pl.ds(ch * CR, CR)
        mid_copy(cross, ch, 0, mp=cross).wait_recv()
        mid_copy(cross, ch, 2, mp=mate).start()
        mid_copy(mate, ch, 1, mp=mate).wait_recv()
        mid_copy(diag, ch, 2, mp=mate).wait_recv()

        @pl.loop(0, CR // RT)
        def _(rt):
            norm_rows(lambda b, r0, n: mid[b, pl.ds(r0, n), :], 1,
                      pl.multiple_of(ch * CR + rt * RT, RT), RT)

        a = nrm[rows, :]
        val = jnp.dot(a, wg[:, pl.ds(0, C)], preferred_element_type=F32)
        gate = jnp.dot(a, wg[:, pl.ds(C, C)], preferred_element_type=F32)
        gated = (val * jax.nn.sigmoid(gate)).astype(BF16).astype(F32)
        for k in range(C // 128):
            ext[k, pl.ds(HALO + ch * CR, CR), :] = gated[:, k * 128:(k + 1) * 128]
        if ch == 0:
            @pl.when(has_left)
            def _():
                halo_left(ext, hg_send, hg_recv).start()

    @pl.when(has_right)
    def _():
        halo_right(ext, hg_send, hg_recv).start()

    @pl.when(has_left)
    def _():
        halo_right(seg_ext, hs_send, hs_recv).wait_recv()
        halo_right(ext, hg_send, hg_recv).wait_recv()

    @pl.when(has_right)
    def _():
        halo_left(seg_ext, hs_send, hs_recv).wait_recv()
        halo_left(ext, hg_send, hg_recv).wait_recv()

    half = (taps - 1) // 2
    for b in range(M):
        loads[4 + 2 * b].wait()
    for ch in range(NCH):
        @pl.loop(0, CR // RT)
        def _(rt):
            r0 = pl.multiple_of(ch * CR + rt * RT, RT)
            here = segcol[pl.ds(r0, RT), :]
            groups = [pl.ds(k * 128, 128) for k in range(C // 128)]
            depth = [jnp.zeros((RT, 128), F32) for _ in groups]
            for j in range(taps):
                at = pl.ds(r0 + (j + HALO - half), RT)
                same = seg_ext[0, at, :] == here
                for k, g in enumerate(groups):
                    depth[k] += jnp.where(same, ext[k, at, :], 0.0) * wdf[pl.ds(j, 1), g]
            for k, g in enumerate(groups):
                z = depth[k] * bns[:, g] + bnb[:, g]
                ctx[pl.ds(r0, RT), g] = (z * jax.nn.sigmoid(z)).astype(BF16)

        scatter_chunk(1, wp, ch)
    for ch in range(NCH):
        rows = pl.ds(ch * CR, CR)
        out[rows, :] = (mid[m, rows, :].astype(F32) + summed(1, ch)).astype(BF16)

    for s in range(T):
        @pl.when(jnp.logical_and(s <= t, t < T - 1))
        def _():
            z_right(s).wait_send()

        @pl.when(jnp.logical_and(s >= t, t > 0))
        def _():
            z_left(s).wait_send()

        over_x(s, m).wait_send()
        to_mate(s, m, 0).wait_send()
        to_mate(s, cross, 1).wait_send()
    for d in range(1, T):
        seg_copy(d).wait_send()

    @pl.when(has_right)
    def _():
        halo_right(seg_ext, hs_send, hs_recv).wait_send()
        halo_right(ext, hg_send, hg_recv).wait_send()

    @pl.when(has_left)
    def _():
        halo_left(seg_ext, hs_send, hs_recv).wait_send()
        halo_left(ext, hg_send, hg_recv).wait_send()

    for ch in range(NCH):
        for ph in range(2):
            rs_a(ph, ch).wait_send()
            rs_x(ph, ch).wait_send()
            rs_b(ph, ch).wait_send()
        mid_copy(m, ch, 0, mp=cross).wait_send()
        mid_copy(m, ch, 1, mp=mate).wait_send()
        mid_copy(cross, ch, 2, mp=mate).wait_send()


def fused_device(
    tokens, segment_ids, ln_att_gain, w_query, w_keyval, w_out, ln_conv_gain, w_glu,
    w_depth, bn_scale, bn_shift, w_proj,
):
    R, C = tokens.shape
    D = ln_att_gain.shape[0]
    T = lax.axis_size("tm")
    M = D // C
    heads = C // HEAD_DIM
    taps = w_depth.shape[0]
    CR = R // NCH
    vmem = pl.BlockSpec(memory_space=pltpu.VMEM)
    hbm = pl.BlockSpec(memory_space=pl.ANY)
    dma = pltpu.SemaphoreType.DMA
    part = pltpu.VMEM((2, NCH, CR, C), BF16)
    return pl.pallas_call(
        functools.partial(block_kernel, T, taps),
        out_shape=jax.ShapeDtypeStruct((R, C), BF16),
        in_specs=[vmem, vmem, vmem, hbm, hbm, hbm, vmem, hbm, vmem, vmem, vmem, hbm],
        out_specs=vmem,
        scratch_shapes=[
            pltpu.VMEM((R, 128), jnp.int32),
            pltpu.VMEM((2, 1, D), F32),
            pltpu.VMEM((1, C), F32),
            pltpu.VMEM((1, C), F32),
            pltpu.VMEM((T, M, R, C), BF16),
            pltpu.VMEM((T, 8, R), jnp.int32),
            pltpu.VMEM((1, R + 2 * HALO, 128), jnp.int32),
            pltpu.VMEM((D, C), BF16),
            pltpu.VMEM((D, 2 * C), BF16),
            pltpu.VMEM((M, C, C), BF16),
            pltpu.VMEM((D, 2 * C), BF16),
            pltpu.VMEM((M, C, C), BF16),
            pltpu.VMEM((R, D), BF16),
            pltpu.VMEM((R, C), BF16),
            pltpu.VMEM((heads * R, C), BF16),
            pltpu.VMEM((heads * R, C), BF16),
            pltpu.VMEM((heads * R, R), F32),
            pltpu.VMEM((R, heads * R), BF16),
            pltpu.VMEM((heads, R, 128), F32),
            pltpu.VMEM((heads, R, 128), F32),
            pltpu.VMEM((R, C), F32),
            pltpu.VMEM((R, C), BF16),
            pltpu.VMEM((R, C), F32),
            pltpu.VMEM((M, R, C), BF16),
            pltpu.VMEM((C // 128, R + 2 * HALO, 128), F32),
            pltpu.VMEM((32, C), F32),
            part, part, part, part, part, part,
            dma((11,)),
            dma((T, M)), dma((2, T)), dma((T,)), dma((T, 2)),
            dma((T,)), dma((T,)), dma((2,)), dma((2,)), dma((2,)), dma((2,)),
            dma((2, NCH, 3)), dma((2, NCH, 3)), dma((NCH, 3)), dma((M, NCH)),
        ],
        compiler_params=pltpu.CompilerParams(
            collective_id=0, has_side_effects=True, vmem_limit_bytes=52 * 2**20
        ),
    )(
        tokens, segment_ids, ln_att_gain, w_query, w_keyval.reshape(D, 2 * C),
        w_out, ln_conv_gain, w_glu.reshape(D, 2 * C), w_depth, bn_scale, bn_shift, w_proj,
    )


def solution(mesh):
    placed = (
        P(("group", "tm"), "mp"),
        P(("group", "tm")),
        P(),
        P(None, "mp"),
        P(None, None, "mp"),
        P("mp", None),
        P(),
        P(None, None, "mp"),
        P(None, "mp"),
        P("mp"),
        P("mp"),
        P("mp", None),
    )
    fused = mesh.shape["tm"] == 4 and mesh.shape["mp"] == 4
    return jax.shard_map(
        fused_device if fused else per_device, mesh=mesh, in_specs=placed, out_specs=P(("group", "tm"), "mp"), check_vma=False
    )
```

```python
import functools

import jax
import jax.numpy as jnp
from jax import lax
from jax.experimental import pallas as pl
from jax.experimental.pallas import tpu as pltpu
from jax.sharding import PartitionSpec as P

HEAD_DIM = 96


def with_halo(value, sides, width):
    for axis, dim in sides:
        count, length = (lax.axis_size(axis), value.shape[dim])
        up = [(i, (i + 1) % count) for i in range(count - 1)]
        down = [(j, i) for i, j in up]
        last = lax.slice_in_dim(value, length - width, length, axis=dim)
        initial = lax.slice_in_dim(value, 0, width, axis=dim)
        before = lax.ppermute(last, axis, up)
        after = lax.ppermute(initial, axis, down)
        value = jnp.concatenate([before, value, after], axis=dim)
    return value


def layer_norm(values_in, gain_vec):
    row_mean = jnp.mean(values_in, axis=-1, keepdims=True)
    centered = values_in - row_mean
    spread = jnp.mean(centered * centered, axis=-1, keepdims=True)
    return centered * lax.rsqrt(spread + 1e-05) * gain_vec


def fold_keys(carry_state, query_heads, query_segs, keyval, key_segs, local_cols, score_scale):
    row_max, weight_sum, weighted = carry_state
    key_rows = keyval.shape[0]
    heads_here = query_heads.shape[1]
    key_part = keyval[:, :local_cols].reshape(key_rows, heads_here, -1)
    value_part = keyval[:, local_cols:].reshape(key_rows, heads_here, -1)
    scores = (
        jnp.einsum("qhd,khd->qhk", query_heads, key_part, preferred_element_type=jnp.float32)
        * score_scale
    )
    same_seg = (query_segs[:, None] == key_segs[None, :])[:, None, :]
    scores = jnp.where(same_seg, scores, -jnp.inf)
    new_max = jnp.maximum(row_max, jnp.max(scores, axis=2))
    safe_max = jnp.where(new_max == -jnp.inf, 0.0, new_max)
    weights = jnp.exp(scores - safe_max[:, :, None])
    factor = jnp.exp(row_max - safe_max)
    weight_sum = weight_sum * factor + jnp.sum(weights, axis=2)
    weighted = weighted * factor[:, :, None] + jnp.einsum(
        "qhk,khd->qhd", weights.astype(jnp.bfloat16), value_part, preferred_element_type=jnp.float32
    )
    return (new_max, weight_sum, weighted)


def maybe_fold(carry_state, query_heads, query_segs, keyval, key_segs, local_cols, score_scale):
    return fold_keys(
        carry_state, query_heads, query_segs, keyval, key_segs, local_cols, score_scale
    )


def per_device(
    tokens,
    segment_ids,
    ln_att_gain,
    w_query,
    w_keyval,
    w_out,
    ln_conv_gain,
    w_glu,
    w_depth,
    bn_scale,
    bn_shift,
    w_proj,
):
    row_count = tokens.shape[0]
    full_width = ln_att_gain.shape[0]
    local_cols = w_query.shape[1]
    heads_here = local_cols // HEAD_DIM
    score_scale = HEAD_DIM ** (-0.5)
    all_segs = lax.all_gather(segment_ids, "tm", axis=0, tiled=True)
    anchor = lax.axis_index("tm") * row_count
    whole_rows = lax.all_gather(tokens, "mp", axis=1, tiled=True)
    normed = layer_norm(whole_rows.astype(jnp.float32), ln_att_gain).astype(jnp.bfloat16)
    queries = jnp.dot(normed, w_query, preferred_element_type=jnp.float32).astype(jnp.bfloat16)
    keyval = jnp.dot(
        normed, w_keyval.reshape(full_width, -1), preferred_element_type=jnp.float32
    ).astype(jnp.bfloat16)
    query_heads = queries.reshape(row_count, heads_here, HEAD_DIM)
    initial = (
        jnp.full((row_count, heads_here), -jnp.inf, jnp.float32),
        jnp.zeros((row_count, heads_here), jnp.float32),
        jnp.zeros((row_count, heads_here, HEAD_DIM), jnp.float32),
    )
    segment = lax.all_gather(keyval, "tm", axis=0, tiled=True)
    piece_rows = segment.shape[0]
    block_count = piece_rows // row_count

    def inner_step(state_in, element):
        return (
            maybe_fold(
                state_in, query_heads, segment_ids, element[0], element[1], local_cols, score_scale
            ),
            None,
        )

    stacked = (
        segment.reshape(block_count, row_count, -1),
        all_segs.reshape(block_count, row_count),
    )
    result, unused = lax.scan(inner_step, initial, stacked)
    row_max, weight_sum, weighted = result
    context = (
        (weighted / weight_sum[:, :, None]).reshape(row_count, local_cols).astype(jnp.bfloat16)
    )
    att_terms = jnp.dot(context, w_out, preferred_element_type=jnp.float32)
    att_summed = lax.psum_scatter(
        att_terms.astype(jnp.bfloat16), "mp", scatter_dimension=1, tiled=True
    ).astype(jnp.float32)
    middle = (tokens.astype(jnp.float32) + att_summed).astype(jnp.bfloat16)
    whole_mid = lax.all_gather(middle, "mp", axis=1, tiled=True)
    normed_conv = layer_norm(whole_mid.astype(jnp.float32), ln_conv_gain).astype(jnp.bfloat16)
    both_halves = jnp.dot(
        normed_conv, w_glu.reshape(full_width, -1), preferred_element_type=jnp.float32
    )
    gated = (both_halves[:, :local_cols] * jax.nn.sigmoid(both_halves[:, local_cols:])).astype(
        jnp.bfloat16
    )
    half_width = (w_depth.shape[0] - 1) // 2
    extended = with_halo(gated, (("tm", 0),), half_width).astype(jnp.float32)
    padded_segs = jnp.pad(all_segs, (half_width, half_width), constant_values=-1)
    window_segs = lax.dynamic_slice_in_dim(padded_segs, anchor, row_count + 2 * half_width, 0)
    depth = jnp.zeros((row_count, local_cols), jnp.float32)
    for tap_index in range(w_depth.shape[0]):
        same_seg = (window_segs[tap_index : tap_index + row_count] == segment_ids)[:, None]
        shifted = jnp.where(same_seg, extended[tap_index : tap_index + row_count], 0.0)
        depth = depth + shifted * w_depth[tap_index].astype(jnp.float32)
    normalized = depth * bn_scale + bn_shift
    swished = (normalized * jax.nn.sigmoid(normalized)).astype(jnp.bfloat16)
    conv_terms = jnp.dot(swished, w_proj, preferred_element_type=jnp.float32)
    conv_summed = lax.psum_scatter(
        conv_terms.astype(jnp.bfloat16), "mp", scatter_dimension=1, tiled=True
    ).astype(jnp.float32)
    return (middle.astype(jnp.float32) + conv_summed).astype(jnp.bfloat16)


NEG = -1e30
HALO = 16
NCH = 2
RS = 128
RN = 96
MESH = pl.DeviceIdType.MESH
F32 = jnp.float32
BF16 = jnp.bfloat16


def block_kernel(
    T, taps,
    tokens, seg, g_att, wq_h, wkv_h, wo_h, g_conv, wg_h, wdep, bn_s, bn_b, wp_h,
    out, segcol, gains, bns, bnb,
    tok, seg_all, seg_ext, wq, wkv, wo, wg, wp, nrm, kbuf, qm, vm, sc, pw, mst, lst, acc,
    ctx, keep, mid, ext, wdf, sa, sx, sb, ra, rx, rb,
    wsem, tok_recv, z_send, x_send, m_send, seg_send, seg_recv, hs_send, hs_recv,
    hg_send, hg_recv, rs_send, rs_recv, mid_send, mid_recv,
):
    R, C = tokens.shape
    M = 4
    D = M * C
    heads = C // HEAD_DIM
    CR = R // NCH
    t = lax.axis_index("tm")
    m = lax.axis_index("mp")
    mate = m + 1 - 2 * (m % 2)
    cross = (m + 2) % 4
    diag = (mate + 2) % 4

    def rcopy(src, dst, ssem, rsem, **dev):
        return pltpu.make_async_remote_copy(
            src_ref=src, dst_ref=dst, send_sem=ssem, recv_sem=rsem,
            device_id=dev, device_id_type=MESH,
        )

    loads = [
        pltpu.make_async_copy(wq_h, wq, wsem.at[0]),
        pltpu.make_async_copy(wkv_h, wkv, wsem.at[1]),
        pltpu.make_async_copy(wg_h, wg, wsem.at[2]),
    ]
    for b in range(M):
        cols = pl.ds(b * C, C)
        loads.append(pltpu.make_async_copy(wo_h.at[:, cols], wo.at[b], wsem.at[3 + b]))
        loads.append(pltpu.make_async_copy(wp_h.at[:, cols], wp.at[b], wsem.at[7 + b]))
    for c in loads:
        c.start()

    barrier = pltpu.get_barrier_semaphore()
    for peer in (mate, cross):
        pl.semaphore_signal(barrier, inc=1, device_id={"mp": peer}, device_id_type=MESH)
    for d in range(1, T):
        pl.semaphore_signal(
            barrier, inc=1, device_id={"tm": (t + d) % T}, device_id_type=MESH
        )
    tok[t, m] = tokens[...]
    ids = seg[...].reshape(1, R)
    seg_all[t] = jnp.broadcast_to(ids, (8, R))
    segcol[...] = jnp.transpose(jnp.broadcast_to(ids, (128, R)))
    seg_ext[0, pl.ds(HALO, R), :] = segcol[...]
    gains[0] = g_att[...].reshape(1, D)
    gains[1] = g_conv[...].reshape(1, D)
    bns[...] = bn_s[...].reshape(1, C)
    bnb[...] = bn_b[...].reshape(1, C)
    pl.semaphore_wait(barrier, 1 + T)

    def z_right(s):
        return rcopy(tok.at[s, m], tok.at[s, m], z_send.at[0, s], tok_recv.at[s, m],
                     tm=(t + 1) % T)

    def z_left(s):
        return rcopy(tok.at[s, m], tok.at[s, m], z_send.at[1, s], tok_recv.at[s, m],
                     tm=(t + T - 1) % T)

    def over_x(s, col):
        return rcopy(tok.at[s, col], tok.at[s, col], x_send.at[s], tok_recv.at[s, col],
                     mp=cross)

    def to_mate(s, col, k):
        return rcopy(tok.at[s, col], tok.at[s, col], m_send.at[s, k], tok_recv.at[s, col],
                     mp=mate)

    def launch(s):
        @pl.when(jnp.logical_and(s <= t, t < T - 1))
        def _():
            z_right(s).start()

        @pl.when(jnp.logical_and(s >= t, t > 0))
        def _():
            z_left(s).start()

        to_mate(s, m, 0).start()

    launch(t)
    over_x(t, m).start()

    def seg_copy(d):
        return rcopy(seg_all.at[t], seg_all.at[t], seg_send.at[d], seg_recv.at[t],
                     tm=(t + d) % T)

    for d in range(1, T):
        seg_copy(d).start()

    def halo_right(ref, ssem, rsem):
        return rcopy(ref.at[:, pl.ds(R, HALO)], ref.at[:, pl.ds(0, HALO)], ssem.at[0],
                     rsem.at[0], tm=(t + 1) % T)

    def halo_left(ref, ssem, rsem):
        return rcopy(ref.at[:, pl.ds(HALO, HALO)], ref.at[:, pl.ds(R + HALO, HALO)],
                     ssem.at[1], rsem.at[1], tm=(t + T - 1) % T)

    has_right = t < T - 1
    has_left = t > 0
    edge = jnp.logical_or(t == 0, t == T - 1)

    @pl.when(has_right)
    def _():
        halo_right(seg_ext, hs_send, hs_recv).start()

    @pl.when(has_left)
    def _():
        halo_left(seg_ext, hs_send, hs_recv).start()

    @pl.when(jnp.logical_not(has_left))
    def _():
        seg_ext[0, pl.ds(0, HALO), :] = jnp.full((HALO, 128), -1, jnp.int32)
        ext[:, pl.ds(0, HALO), :] = jnp.zeros((C // 128, HALO, 128), F32)

    @pl.when(jnp.logical_not(has_right))
    def _():
        seg_ext[0, pl.ds(R + HALO, HALO), :] = jnp.full((HALO, 128), -1, jnp.int32)
        ext[:, pl.ds(R + HALO, HALO), :] = jnp.zeros((C // 128, HALO, 128), F32)

    wdf[pl.ds(0, taps), :] = wdep[...].astype(F32)
    mst[...] = jnp.full(mst.shape, NEG, F32)
    lst[...] = jnp.zeros(lst.shape, F32)
    acc[...] = jnp.zeros(acc.shape, F32)
    head_of = lax.broadcasted_iota(jnp.int32, (1, C), 1) // HEAD_DIM

    def norm_rows(load, gain, r0, n):
        parts = [load(b, r0, n).astype(F32) for b in range(M)]
        total = parts[0] + parts[1] + parts[2] + parts[3]
        mean = jnp.sum(total, axis=1, keepdims=True) * (1.0 / D)
        parts = [p - mean for p in parts]
        sq = parts[0] * parts[0]
        for p in parts[1:]:
            sq = sq + p * p
        inv = lax.rsqrt(jnp.sum(sq, axis=1, keepdims=True) * (1.0 / D) + 1e-05)
        for b in range(M):
            nrm[pl.ds(r0, n), pl.ds(b * C, C)] = (
                parts[b] * inv * gains[gain, :, pl.ds(b * C, C)]
            ).astype(BF16)

    RT = 32
    coef = float(HEAD_DIM ** (-0.5))

    def fold(x):
        return sum(x[:, k * 128:(k + 1) * 128] for k in range(1, C // 128)) + x[:, :128]

    def wide(col):
        return jnp.concatenate([col] * (C // 128), axis=1)

    def softmax_rows(s, rt):
        r0 = pl.multiple_of(rt * RS, RS)
        rows = pl.ds(r0, RS)
        bias = jnp.where(wide(segcol[rows, :]) == seg_all[s, pl.ds(0, 1), :], 0.0, NEG)
        hs = range(heads)
        xs = [sc[pl.ds(pl.multiple_of(h * R + r0, RS), RS), :] + bias for h in hs]
        olds = [mst[h, rows, :] for h in hs]
        sums = [lst[h, rows, :] for h in hs]
        news = [jnp.maximum(o, jnp.max(x, axis=1, keepdims=True)) for o, x in zip(olds, xs)]
        fs = [jnp.exp((o - n) * coef) for o, n in zip(olds, news)]
        ps = [jnp.exp((x - wide(n)) * coef) for x, n in zip(xs, news)]
        sums = [v * f + fold(p) for v, f, p in zip(sums, fs, ps)]
        lanes = wide(fs[0])
        for h in hs[1:]:
            lanes = jnp.where(head_of == h, wide(fs[h]), lanes)
        for h in hs:
            mst[h, rows, :] = news[h]
            lst[h, rows, :] = sums[h]
            pw[rows, pl.ds(h * R, R)] = ps[h].astype(BF16)
        acc[rows, :] = acc[rows, :] * lanes

    def block_step(i, code):
        s = code % T
        nxt = (code // T) % T
        after = (code // (T * T)) % T

        @pl.when(jnp.logical_or(i == 0, jnp.logical_and(edge, i + 1 < T)))
        def _():
            z_right(nxt).wait_recv()
            launch(nxt)

        @pl.when(jnp.logical_and(jnp.logical_not(edge), i < 2))
        def _():
            z_right(after).wait_recv()
            launch(after)

        @pl.when(i + 1 < T)
        def _():
            over_x(nxt, m).start()

        over_x(s, cross).wait_recv()
        to_mate(s, cross, 1).start()
        to_mate(s, mate, 0).wait_recv()
        to_mate(s, diag, 1).wait_recv()

        @pl.when(i == 0)
        def _():
            loads[0].wait()
            loads[1].wait()

        @pl.when(i > 0)
        def _():
            rcopy(seg_all.at[s], seg_all.at[s], seg_send.at[0], seg_recv.at[s],
                  tm=(t + 1) % T).wait_recv()

        @pl.loop(0, R // RN)
        def _(rt):
            norm_rows(lambda b, r0, n: tok[s, b, pl.ds(r0, n), :], 0,
                      pl.multiple_of(rt * RN, RN), RN)

        @pl.when(i == 0)
        def _():
            q = jnp.dot(nrm[...], wq[...], preferred_element_type=F32).astype(BF16)
            for h in range(heads):
                qm[pl.ds(h * R, R), :] = jnp.where(head_of == h, q, jnp.zeros_like(q))

        kbuf[...] = jnp.dot(
            nrm[...], wkv[:, pl.ds(0, C)], preferred_element_type=F32).astype(BF16)
        v = jnp.dot(nrm[...], wkv[:, pl.ds(C, C)], preferred_element_type=F32).astype(BF16)
        for h in range(heads):
            vm[pl.ds(h * R, R), :] = jnp.where(head_of == h, v, jnp.zeros_like(v))
        for h in range(heads):
            sc[pl.ds(h * R, R), :] = lax.dot_general(
                qm[pl.ds(h * R, R), :], kbuf[...], (((1,), (1,)), ((), ())),
                preferred_element_type=F32)

        @pl.loop(0, R // RS)
        def _(rt):
            softmax_rows(s, rt)

        acc[...] += jnp.dot(pw[...], vm[...], preferred_element_type=F32)
        return code // T

    order = 228 - 3 * ((t + 3) // 4) - 171 * ((t + 2) // 4) - 27 * ((t + 1) // 4)
    lax.fori_loop(0, T, block_step, order)

    den = None
    for h in range(heads):
        col = jnp.sum(lst[h, :, :], axis=1, keepdims=True)
        den = col if den is None else jnp.where(head_of == h, col, den)
    ctx[...] = (acc[...] / den).astype(BF16)

    def rs_a(ph, ch):
        return rcopy(sa.at[ph, ch], ra.at[ph, ch], rs_send.at[ph, ch, 0],
                     rs_recv.at[ph, ch, 0], mp=mate)

    def rs_x(ph, ch):
        return rcopy(sx.at[ph, ch], rx.at[ph, ch], rs_send.at[ph, ch, 1],
                     rs_recv.at[ph, ch, 1], mp=cross)

    def rs_b(ph, ch):
        return rcopy(sb.at[ph, ch], rb.at[ph, ch], rs_send.at[ph, ch, 2],
                     rs_recv.at[ph, ch, 2], mp=mate)

    def scatter_chunk(ph, w, ch):
        a = ctx[pl.ds(ch * CR, CR), :]
        sa[ph, ch] = jnp.dot(a, w[diag], preferred_element_type=F32).astype(BF16)
        rs_a(ph, ch).start()
        mine = jnp.dot(a, w[cross], preferred_element_type=F32)
        sb[ph, ch] = jnp.dot(a, w[mate], preferred_element_type=F32).astype(BF16)
        rs_b(ph, ch).start()
        rs_a(ph, ch).wait_recv()
        sx[ph, ch] = (mine + ra[ph, ch].astype(F32)).astype(BF16)
        rs_x(ph, ch).start()
        keep[pl.ds(ch * CR, CR), :] = (
            jnp.dot(a, w[m], preferred_element_type=F32).astype(BF16).astype(F32))

    def summed(ph, ch):
        rs_b(ph, ch).wait_recv()
        rs_x(ph, ch).wait_recv()
        return (keep[pl.ds(ch * CR, CR), :] + rb[ph, ch].astype(F32)) + rx[ph, ch].astype(F32)

    for b in range(M):
        loads[3 + 2 * b].wait()
    for ch in range(NCH):
        scatter_chunk(0, wo, ch)

    def mid_copy(col, ch, k, **dev):
        piece = mid.at[col, pl.ds(ch * CR, CR)]
        return rcopy(piece, piece, mid_send.at[ch, k], mid_recv.at[col, ch], **dev)

    for ch in range(NCH):
        rows = pl.ds(ch * CR, CR)
        mid[m, rows, :] = (tokens[rows, :].astype(F32) + summed(0, ch)).astype(BF16)
        mid_copy(m, ch, 0, mp=cross).start()
        mid_copy(m, ch, 1, mp=mate).start()
    loads[2].wait()
    for ch in range(NCH):
        rows = pl.ds(ch * CR, CR)
        mid_copy(cross, ch, 0, mp=cross).wait_recv()
        mid_copy(cross, ch, 2, mp=mate).start()
        mid_copy(mate, ch, 1, mp=mate).wait_recv()
        mid_copy(diag, ch, 2, mp=mate).wait_recv()

        @pl.loop(0, CR // RN)
        def _(rt):
            norm_rows(lambda b, r0, n: mid[b, pl.ds(r0, n), :], 1,
                      pl.multiple_of(ch * CR + rt * RN, RN), RN)

        a = nrm[rows, :]
        val = jnp.dot(a, wg[:, pl.ds(0, C)], preferred_element_type=F32)
        gate = jnp.dot(a, wg[:, pl.ds(C, C)], preferred_element_type=F32)
        gated = (val * jax.nn.sigmoid(gate)).astype(BF16).astype(F32)
        for k in range(C // 128):
            ext[k, pl.ds(HALO + ch * CR, CR), :] = gated[:, k * 128:(k + 1) * 128]
        if ch == 0:
            @pl.when(has_left)
            def _():
                halo_left(ext, hg_send, hg_recv).start()

    @pl.when(has_right)
    def _():
        halo_right(ext, hg_send, hg_recv).start()

    @pl.when(has_left)
    def _():
        halo_right(seg_ext, hs_send, hs_recv).wait_recv()
        halo_right(ext, hg_send, hg_recv).wait_recv()

    @pl.when(has_right)
    def _():
        halo_left(seg_ext, hs_send, hs_recv).wait_recv()
        halo_left(ext, hg_send, hg_recv).wait_recv()

    half = (taps - 1) // 2
    for b in range(M):
        loads[4 + 2 * b].wait()
    for ch in range(NCH):
        @pl.loop(0, CR // RT)
        def _(rt):
            r0 = pl.multiple_of(ch * CR + rt * RT, RT)
            here = segcol[pl.ds(r0, RT), :]
            groups = [pl.ds(k * 128, 128) for k in range(C // 128)]
            depth = [jnp.zeros((RT, 128), F32) for _ in groups]
            for j in range(taps):
                at = pl.ds(r0 + (j + HALO - half), RT)
                same = seg_ext[0, at, :] == here
                for k, g in enumerate(groups):
                    depth[k] += jnp.where(same, ext[k, at, :], 0.0) * wdf[pl.ds(j, 1), g]
            for k, g in enumerate(groups):
                z = depth[k] * bns[:, g] + bnb[:, g]
                ctx[pl.ds(r0, RT), g] = (z * jax.nn.sigmoid(z)).astype(BF16)

        scatter_chunk(1, wp, ch)
    for ch in range(NCH):
        rows = pl.ds(ch * CR, CR)
        out[rows, :] = (mid[m, rows, :].astype(F32) + summed(1, ch)).astype(BF16)

    for s in range(T):
        @pl.when(jnp.logical_and(s <= t, t < T - 1))
        def _():
            z_right(s).wait_send()

        @pl.when(jnp.logical_and(s >= t, t > 0))
        def _():
            z_left(s).wait_send()

        over_x(s, m).wait_send()
        to_mate(s, m, 0).wait_send()
        to_mate(s, cross, 1).wait_send()
    for d in range(1, T):
        seg_copy(d).wait_send()

    @pl.when(has_right)
    def _():
        halo_right(seg_ext, hs_send, hs_recv).wait_send()
        halo_right(ext, hg_send, hg_recv).wait_send()

    @pl.when(has_left)
    def _():
        halo_left(seg_ext, hs_send, hs_recv).wait_send()
        halo_left(ext, hg_send, hg_recv).wait_send()

    for ch in range(NCH):
        for ph in range(2):
            rs_a(ph, ch).wait_send()
            rs_x(ph, ch).wait_send()
            rs_b(ph, ch).wait_send()
        mid_copy(m, ch, 0, mp=cross).wait_send()
        mid_copy(m, ch, 1, mp=mate).wait_send()
        mid_copy(cross, ch, 2, mp=mate).wait_send()


def fused_device(
    tokens, segment_ids, ln_att_gain, w_query, w_keyval, w_out, ln_conv_gain, w_glu,
    w_depth, bn_scale, bn_shift, w_proj,
):
    R, C = tokens.shape
    D = ln_att_gain.shape[0]
    T = lax.axis_size("tm")
    M = D // C
    heads = C // HEAD_DIM
    taps = w_depth.shape[0]
    CR = R // NCH
    vmem = pl.BlockSpec(memory_space=pltpu.VMEM)
    hbm = pl.BlockSpec(memory_space=pl.ANY)
    dma = pltpu.SemaphoreType.DMA
    part = pltpu.VMEM((2, NCH, CR, C), BF16)
    return pl.pallas_call(
        functools.partial(block_kernel, T, taps),
        out_shape=jax.ShapeDtypeStruct((R, C), BF16),
        in_specs=[vmem, vmem, vmem, hbm, hbm, hbm, vmem, hbm, vmem, vmem, vmem, hbm],
        out_specs=vmem,
        scratch_shapes=[
            pltpu.VMEM((R, 128), jnp.int32),
            pltpu.VMEM((2, 1, D), F32),
            pltpu.VMEM((1, C), F32),
            pltpu.VMEM((1, C), F32),
            pltpu.VMEM((T, M, R, C), BF16),
            pltpu.VMEM((T, 8, R), jnp.int32),
            pltpu.VMEM((1, R + 2 * HALO, 128), jnp.int32),
            pltpu.VMEM((D, C), BF16),
            pltpu.VMEM((D, 2 * C), BF16),
            pltpu.VMEM((M, C, C), BF16),
            pltpu.VMEM((D, 2 * C), BF16),
            pltpu.VMEM((M, C, C), BF16),
            pltpu.VMEM((R, D), BF16),
            pltpu.VMEM((R, C), BF16),
            pltpu.VMEM((heads * R, C), BF16),
            pltpu.VMEM((heads * R, C), BF16),
            pltpu.VMEM((heads * R, R), F32),
            pltpu.VMEM((R, heads * R), BF16),
            pltpu.VMEM((heads, R, 128), F32),
            pltpu.VMEM((heads, R, 128), F32),
            pltpu.VMEM((R, C), F32),
            pltpu.VMEM((R, C), BF16),
            pltpu.VMEM((R, C), F32),
            pltpu.VMEM((M, R, C), BF16),
            pltpu.VMEM((C // 128, R + 2 * HALO, 128), F32),
            pltpu.VMEM((32, C), F32),
            part, part, part, part, part, part,
            dma((11,)),
            dma((T, M)), dma((2, T)), dma((T,)), dma((T, 2)),
            dma((T,)), dma((T,)), dma((2,)), dma((2,)), dma((2,)), dma((2,)),
            dma((2, NCH, 3)), dma((2, NCH, 3)), dma((NCH, 3)), dma((M, NCH)),
        ],
        compiler_params=pltpu.CompilerParams(
            collective_id=0, has_side_effects=True, vmem_limit_bytes=52 * 2**20
        ),
    )(
        tokens, segment_ids, ln_att_gain, w_query, w_keyval.reshape(D, 2 * C),
        w_out, ln_conv_gain, w_glu.reshape(D, 2 * C), w_depth, bn_scale, bn_shift, w_proj,
    )


def solution(mesh):
    placed = (
        P(("group", "tm"), "mp"),
        P(("group", "tm")),
        P(),
        P(None, "mp"),
        P(None, None, "mp"),
        P("mp", None),
        P(),
        P(None, None, "mp"),
        P(None, "mp"),
        P("mp"),
        P("mp"),
        P("mp", None),
    )
    fused = mesh.shape["tm"] == 4 and mesh.shape["mp"] == 4
    return jax.shard_map(
        fused_device if fused else per_device, mesh=mesh, in_specs=placed, out_specs=P(("group", "tm"), "mp"), check_vma=False
    )
```
